32 devices in a mesh: dp: 4 (over x, core), fsdp: 8 (over z, y).
Axes of the slice: x: 2, y: 2, z: 4, core: 2. Of those that a mesh axis runs over, the one named last changes fastest.
Arguments:
- layer_in: bfloat16 [2, 8, 1536, 896], P(None, 'fsdp', 'dp'), may hold values from -16 to 16
- cotangent: bfloat16 [2, 8, 1536, 896], P(None, 'fsdp', 'dp'), may hold values from -6 to 6
- block_doc: int32 [2, 8, 12], P(None, 'fsdp'), may hold values from 0 to 1, as said below
- query_weight: bfloat16 [896, 896], P(('dp', 'fsdp')), may hold values from -0.1875 to 0.1875
- key_weight: bfloat16 [896, 128], P(('dp', 'fsdp')), may hold values from -0.1875 to 0.1875
- value_weight: bfloat16 [896, 128], P(('dp', 'fsdp')), may hold values from -0.1875 to 0.1875
- output_weight: bfloat16 [896, 896], P(('dp', 'fsdp')), may hold values from -0.75 to 0.75
- gate_weight: bfloat16 [896, 4864], P(('dp', 'fsdp')), may hold values from -0.1875 to 0.1875
- up_weight: bfloat16 [896, 4864], P(('dp', 'fsdp')), may hold values from -0.1875 to 0.1875
- down_weight: bfloat16 [4864, 896], P(('dp', 'fsdp')), may hold values from -0.078125 to 0.078125
- query_bias: bfloat16 [896], P(('dp', 'fsdp')), may hold values from -0.5 to 0.5
- key_bias: bfloat16 [128], P(('dp', 'fsdp')), may hold values from -0.5 to 0.5
- value_bias: bfloat16 [128], P(('dp', 'fsdp')), may hold values from -0.5 to 0.5
- norm_one: bfloat16 [896], P(('dp', 'fsdp')), may hold values from 0.5 to 1.5
- norm_two: bfloat16 [896], P(('dp', 'fsdp')), may hold values from 0.5 to 1.5
Outputs:
- layer_out: bfloat16 [2, 8, 1536, 896], P(None, 'fsdp', 'dp')
- input_grad: float32 [2, 8, 1536, 896], P(None, 'fsdp', 'dp')
- query_weight_grad: float32 [896, 896], P(('dp', 'fsdp'))
- key_weight_grad: float32 [896, 128], P(('dp', 'fsdp'))
- value_weight_grad: float32 [896, 128], P(('dp', 'fsdp'))
- output_weight_grad: float32 [896, 896], P(('dp', 'fsdp'))
- gate_weight_grad: float32 [896, 4864], P(('dp', 'fsdp'))
- up_weight_grad: float32 [896, 4864], P(('dp', 'fsdp'))
- down_weight_grad: float32 [4864, 896], P(('dp', 'fsdp'))
- query_bias_grad: float32 [896], P(('dp', 'fsdp'))
- key_bias_grad: float32 [128], P(('dp', 'fsdp'))
- value_bias_grad: float32 [128], P(('dp', 'fsdp'))
- norm_one_grad: float32 [896], P(('dp', 'fsdp'))
- norm_two_grad: float32 [896], P(('dp', 'fsdp'))
The draws below stay inside these ranges and needn't reach their ends.
Inputs may be any that keep to these rules, and one draw needn't show every extreme that they name: Each stream holds one sequence: block_doc is 0 on its first L blocks and 1 (padding) on the rest, with L from 8 to 12; some stream has L = 12 and some L = 8.
All inputs are finite; a program needn't handle non-finite values.
Results may differ from the reference program's by a relative error of at most 0.03.
Values may be sent and summed in bfloat16 or wider, within the bound.
No kernel may reach another device: no remote copies, remote signals or barrier semaphores. Data moves between devices by JAX's collectives and lax.ppermute only.
A program may use at most 256 MiB of HBM per device.

```python
import math
import jax
import jax.numpy as jnp
from jax import lax

D = 896
H = 14
KVH = 2
HD = 64
FF = 4864
M = 2
TOK_MB = 384
BLK = 128
MIN_BLK = 8
GRP = 8
STREAM = 1536
NBLK = 12


def draw_layer_in(key, part):
    subkeys = jax.random.split(key, 4)
    device_count = STREAM // TOK_MB * GRP
    row_draw = jax.random.uniform(subkeys[0], (M, GRP, STREAM, 1))
    row_scale = 0.4 * jnp.exp(row_draw * jnp.log(6.25))
    col_draw = jax.random.uniform(subkeys[1], (1, 1, 1, D))
    col_scale = 0.6 * jnp.exp(col_draw * jnp.log(2.6667))
    pairing = jax.random.permutation(subkeys[2], device_count)
    owner = (jnp.arange(STREAM) // TOK_MB)[None, :] * GRP + jnp.arange(GRP)[:, None]
    target = pairing[owner]
    column_block = jnp.arange(D) // (D // device_count)
    spike = jnp.where(target[:, :, None] == column_block[None, None, :], 3.0, 1.0)[None]
    base_draw = jax.random.truncated_normal(subkeys[3], -4.0, 4.0, (M, GRP, STREAM, D))
    values = jnp.clip(base_draw * row_scale * col_scale * spike, -16.0, 16.0)
    return values.astype(jnp.float32).astype(jnp.bfloat16)


def draw_block_doc(key, part):
    seq_blocks = jax.random.randint(key, (M, GRP, 1), MIN_BLK, NBLK + 1)
    seq_blocks = seq_blocks.at[0, 0, 0].set(NBLK).at[0, 1, 0].set(MIN_BLK)
    blocks = jnp.arange(NBLK, dtype=jnp.int32)[None, None, :]
    return (blocks >= seq_blocks).astype(jnp.int32)


def block_scale(stream_key, dims, cuts, least, top_value):
    level = 1.0
    for axis_at, shards_of in cuts:
        heights = jax.random.uniform(jax.random.fold_in(jax.random.fold_in(stream_key, 6), axis_at), (shards_of,), jnp.float32, least / len(cuts), top_value / len(cuts))
        level = level * jnp.repeat(jnp.exp(heights), dims[axis_at] // shards_of).reshape((-1,) + (1,) * (len(dims) - 1 - axis_at))
    return level


def noise(rng, extent, scale, limit, cuts=(), held_as=jnp.bfloat16):
    array = jax.random.normal(rng, extent, jnp.float32) * scale
    if len(cuts) > 0:
        array = block_scale(rng, extent, cuts, -0.22, 0.18) * array
    return jnp.clip(array, min=-limit, max=limit).astype(held_as)


def setup_inputs(seed: int = 0) -> dict:
    streams_of = jax.random.split(jax.random.key(seed), 16)
    layer_in = draw_layer_in(jax.random.fold_in(streams_of[15], 71), 0)
    cotangent = noise(streams_of[1], (M, GRP, STREAM, D), 1.0, 6.0, ((1, 8), (2, 4)))
    block_doc = draw_block_doc(jax.random.fold_in(streams_of[15], 71), 0)
    query_weight = noise(streams_of[3], (D, H * HD), D ** -0.5, 0.1875, ((0, 32),))
    key_weight = noise(streams_of[4], (D, KVH * HD), D ** -0.5, 0.1875, ((0, 32),))
    value_weight = noise(streams_of[5], (D, KVH * HD), D ** -0.5, 0.1875, ((0, 32),))
    output_weight = noise(streams_of[6], (H * HD, D), (H * HD // 16) ** -0.5, 0.75, ((0, 32),))
    gate_weight = noise(streams_of[7], (D, FF), D ** -0.5, 0.1875, ((0, 32),))
    up_weight = noise(streams_of[8], (D, FF), D ** -0.5, 0.1875, ((0, 32),))
    down_weight = noise(streams_of[9], (FF, D), FF ** -0.5, 0.078125, ((0, 32),))
    query_bias = jnp.clip(jax.random.uniform(streams_of[10], (H * HD,), jnp.float32, -0.5, 0.5) * block_scale(streams_of[10], (H * HD,), ((0, 32),), -0.4, 0.0), -0.5, 0.5).astype(jnp.bfloat16)
    key_bias = jnp.clip(jax.random.uniform(streams_of[11], (KVH * HD,), jnp.float32, -0.5, 0.5) * block_scale(streams_of[11], (KVH * HD,), ((0, 32),), -0.4, 0.0), -0.5, 0.5).astype(jnp.bfloat16)
    value_bias = jnp.clip(jax.random.uniform(streams_of[12], (KVH * HD,), jnp.float32, -0.5, 0.5) * block_scale(streams_of[12], (KVH * HD,), ((0, 32),), -0.4, 0.0), -0.5, 0.5).astype(jnp.bfloat16)
    norm_one = jnp.clip(1.0 + 0.1 * jax.random.normal(streams_of[13], (D,), jnp.float32), 0.5, 1.5).astype(jnp.bfloat16)
    norm_two = jnp.clip(1.0 + 0.1 * jax.random.normal(streams_of[14], (D,), jnp.float32), 0.5, 1.5).astype(jnp.bfloat16)
    return {"layer_in": layer_in, "cotangent": cotangent, "block_doc": block_doc, "query_weight": query_weight, "key_weight": key_weight, "value_weight": value_weight, "output_weight": output_weight, "gate_weight": gate_weight, "up_weight": up_weight, "down_weight": down_weight, "query_bias": query_bias, "key_bias": key_bias, "value_bias": value_bias, "norm_one": norm_one, "norm_two": norm_two}


@jax.custom_vjp
def low(v):
    return lax.optimization_barrier(v.astype(jnp.bfloat16)).astype(jnp.float32)

@jax.custom_vjp
def low_back(v):
    return v

def low_keep(v):
    return (low(v), None)

def low_pass(kept, grad):
    return (grad,)

def back_keep(v):
    return (v, None)

def back_low(kept, grad):
    return (low(grad),)
low.defvjp(low_keep, low_pass)
low_back.defvjp(back_keep, back_low)
EPSILON = 1e-06
THETA = 1000000.0

def matmul(left, right):
    return jnp.dot(left, right, precision=lax.Precision.HIGHEST)

def rms_norm(vectors, gain_vec):
    return vectors * lax.rsqrt(lax.optimization_barrier(jnp.mean(vectors * vectors, axis=-1, keepdims=True)) + EPSILON) * gain_vec

def stream_positions(block_ids):
    lower_count = lax.optimization_barrier(jnp.sum((block_ids[None, :] < block_ids[:, None]).astype(jnp.int32), axis=1))
    tokens = jnp.arange(block_ids.shape[0] * BLK, dtype=jnp.int32)
    first_tok = jnp.repeat(lower_count, BLK) * BLK
    return ((tokens - first_tok).astype(jnp.float32), jnp.repeat(block_ids, BLK))

def rotate(vectors, position):
    half_dim = HD // 2
    frequency = jnp.exp(jnp.arange(half_dim, dtype=jnp.float32) * (-2.0 * math.log(THETA) / HD))
    angles = position[:, None] * frequency[None, :]
    cosine = jnp.cos(angles)[:, None, :]
    sine_of = jnp.sin(angles)[:, None, :]
    first_half = vectors[..., :half_dim]
    second_half = vectors[..., half_dim:]
    return jnp.concatenate([first_half * cosine - second_half * sine_of, second_half * cosine + first_half * sine_of], axis=-1)

def stream_layer(x_rows, block_ids, params):
    w_query, w_key, w_value, w_output, w_gate, w_upward, w_down, b_query, b_key, b_value, gain_one, gain_two = params
    length = x_rows.shape[0]
    position, token_doc = stream_positions(block_ids)
    normed = low(rms_norm(x_rows, gain_one))
    query_pre = low_back(matmul(normed, w_query) + b_query)
    key_pre = low_back(matmul(normed, w_key) + b_key)
    values = low(low_back(matmul(normed, w_value) + b_value)).reshape(length, KVH, HD)
    queries = low(rotate(query_pre.reshape(length, H, HD), position)).reshape(length, KVH, H // KVH, HD)
    key_rot = low(rotate(key_pre.reshape(length, KVH, HD), position))
    scores = low_back(jnp.einsum('qkgd,nkd->kgqn', queries, key_rot, precision=lax.Precision.HIGHEST) * HD ** (-0.5))
    indices = jnp.arange(length, dtype=jnp.int32)
    allowed = (token_doc[:, None] == token_doc[None, :]) & (indices[None, :] <= indices[:, None])
    weights = low(jax.nn.softmax(jnp.where(allowed, scores, -jnp.inf), axis=-1))
    attended = jnp.einsum('kgqn,nkd->qkgd', weights, values, precision=lax.Precision.HIGHEST).reshape(length, H * HD)
    attended = low(low_back(attended))
    middle = x_rows + low_back(matmul(attended, w_output))
    normed_two = low(rms_norm(middle, gain_two))
    gate_pre = low_back(matmul(normed_two, w_gate))
    upward = low_back(matmul(normed_two, w_upward))
    hidden = low(jax.nn.silu(gate_pre) * upward)
    return middle + matmul(hidden, w_down)

def reference(layer_in, cotangent, block_doc, query_weight, key_weight, value_weight, output_weight, gate_weight, up_weight, down_weight, query_bias, key_bias, value_bias, norm_one, norm_two):
    params = tuple((matrix.astype(jnp.float32) for matrix in (query_weight, key_weight, value_weight, output_weight, gate_weight, up_weight, down_weight, query_bias, key_bias, value_bias, norm_one, norm_two)))
    streams = layer_in.astype(jnp.float32).reshape(M * GRP, STREAM, D)
    stream_docs = block_doc.reshape(M * GRP, NBLK)

    def forward(inputs, weights_all):

        def single(paired):
            return jax.checkpoint(stream_layer)(paired[0], paired[1], weights_all)
        return lax.map(single, (inputs, stream_docs))
    outputs, pullback = jax.vjp(forward, streams, params)
    grad_x, grad_all = pullback(cotangent.astype(jnp.float32).reshape(M * GRP, STREAM, D))
    return (outputs.reshape(M, GRP, STREAM, D).astype(jnp.bfloat16), grad_x.reshape(M, GRP, STREAM, D), grad_all[0], grad_all[1], grad_all[2], grad_all[3], grad_all[4], grad_all[5], grad_all[6], grad_all[7], grad_all[8], grad_all[9], grad_all[10], grad_all[11])
```

```python
import functools
import jax, jax.numpy as jnp
from jax import lax
from jax.experimental import pallas as pl
from jax.experimental.pallas import tpu as pltpu
BF=jnp.bfloat16; F32=jnp.float32
NT=(((1,),(1,)),((),())); NN=(((1,),(0,)),((),())); TN=(((0,),(0,)),((),()))
H=14; KVH=2; HD=64; G=7; BLK=128
NEG=-1e30
def dot(a,b,d): return lax.dot_general(a,b,d,preferred_element_type=F32)
CH=256
def fill_bias(meta, bias_ref, tq, npc):
    q0=meta[0]; lim=meta[1]
    for ph in range(3):
        col=lax.broadcasted_iota(jnp.int32,(1,CH),1)+ph*CH
        col=jnp.where(col>=tq, col-tq, col)
        q=q0+col
        start=jnp.where(q>=lim, lim, 0)
        for p in range(npc):
            k=meta[2+p]+lax.broadcasted_iota(jnp.int32,(tq,1),0)
            ok=(k>=start)&(k<=q)
            bias_ref[ph,p*tq:(p+1)*tq,:]=jnp.where(ok,0.0,NEG)
def fwd_kernel(meta, x_ref, qT_ref, kv0, kv1, kv2, kv3, wo_ref, g2_ref, oT_ref, lse_ref, att_ref, mid_ref, h2_ref,
               bias_ref, k_ref, vT_ref, s_ref):
    tq=x_ref.shape[0]; kvs=(kv0,kv1,kv2,kv3); npc=4; nk=npc*tq
    nch=qT_ref.shape[2]//CH
    fill_bias(meta,bias_ref,tq,npc)
    for p in range(npc):
        kv=kvs[p][...]
        vt=kv[:,128:].T
        for j in range(KVH):
            k_ref[j,p*tq:(p+1)*tq,:]=kv[:,j*HD:(j+1)*HD]
            vT_ref[j,:,p*tq:(p+1)*tq]=vt[j*HD:(j+1)*HD,:]
    def body(i, _):
        j=i//nch; c=i%nch
        ph=lax.rem(c,3)
        cs=pl.ds(pl.multiple_of(c*CH,CH),CH)
        q=qT_ref[j,:,cs]
        m=jnp.full((1,CH),NEG,F32)
        for p in range(npc):
            s=dot(k_ref[j,p*tq:(p+1)*tq,:],q,NN)+bias_ref[ph,p*tq:(p+1)*tq,:]
            s_ref[p*tq:(p+1)*tq,:]=s
            m=jnp.maximum(m,jnp.max(s,axis=0,keepdims=True))
        l=jnp.zeros((1,CH),F32); acc=jnp.zeros((HD,CH),F32)
        for p in range(npc):
            e=jnp.exp(s_ref[p*tq:(p+1)*tq,:]-m)
            l=l+jnp.sum(e,axis=0,keepdims=True)
            acc=acc+dot(vT_ref[j,:,p*tq:(p+1)*tq],e.astype(BF),NN)
        oT_ref[j,:,cs]=acc*(1.0/l)
        lse_ref[j,:,cs]=m+jnp.log(l)
        return 0
    lax.fori_loop(0,KVH*nch,body,0)
    for h in range(H):
        j,i=h//G,h%G
        att_ref[:,h*HD:(h+1)*HD]=oT_ref[j,:,i*tq:(i+1)*tq].T.astype(BF)
    mid=x_ref[...].astype(F32)+dot(att_ref[...],wo_ref[...],NN)
    mid_ref[...]=mid
    r=lax.rsqrt(jnp.mean(mid*mid,axis=1,keepdims=True)+1e-6)
    h2_ref[...]=(mid*r*g2_ref[...]).astype(BF)
def attn_fwd(meta,x,qT,kvs,wo,g2):
    tq=x.shape[0]; D=x.shape[1]; W=qT.shape[2]
    vm=pl.BlockSpec(memory_space=pltpu.VMEM)
    return pl.pallas_call(fwd_kernel,
        in_specs=[pl.BlockSpec(memory_space=pltpu.SMEM)]+[vm]*8, out_specs=[vm]*5,
        out_shape=[jax.ShapeDtypeStruct((KVH,HD,W),F32),jax.ShapeDtypeStruct((KVH,1,W),F32),
                   jax.ShapeDtypeStruct((tq,D),BF),jax.ShapeDtypeStruct((tq,D),F32),jax.ShapeDtypeStruct((tq,D),BF)],
        scratch_shapes=[pltpu.VMEM((3,4*tq,CH),F32),pltpu.VMEM((KVH,4*tq,HD),BF),pltpu.VMEM((KVH,HD,4*tq),BF),pltpu.VMEM((4*tq,CH),F32)],
        compiler_params=pltpu.CompilerParams(vmem_limit_bytes=56<<20), name="attn_fwd")(meta,x,qT,*kvs,wo,g2)
def bwd_kernel(meta, mid_ref, c_ref, dh_ref, qT_ref, kv0, kv1, kv2, kv3, oT_ref, lse_ref, wo_ref, g2_ref, cos_ref, sin_ref,
               dmid_ref, dbr_ref, dq_ref, da_ref, db_ref, dg2_ref,
               bias_ref, k_ref, v_ref, kT_ref, doT_ref, dqT_ref, dk_ref, dv_ref):
    tq=mid_ref.shape[0]; kvs=(kv0,kv1,kv2,kv3); npc=4
    nch=qT_ref.shape[2]//CH
    mid=mid_ref[...]; e=dh_ref[...]
    r=lax.rsqrt(jnp.mean(mid*mid,axis=1,keepdims=True)+1e-6)
    sc=e*g2_ref[...]
    inner=jnp.mean(sc*mid,axis=1,keepdims=True)
    dmid=c_ref[...].astype(F32)+r*sc-mid*(r*r*r)*inner
    dmid_ref[...]=dmid
    dg2_ref[...]=jnp.sum(e*mid*r,axis=0,keepdims=True)
    dbr=dmid.astype(BF)
    dbr_ref[...]=dbr
    datT=dot(wo_ref[...],dbr,NT).astype(BF)
    for h in range(H):
        j,i=h//G,h%G
        doT_ref[j,:,i*tq:(i+1)*tq]=datT[h*HD:(h+1)*HD,:]
    pad=qT_ref.shape[2]-G*tq
    if pad:
        for j in range(KVH): doT_ref[j,:,G*tq:]=jnp.zeros((HD,pad),BF)
    fill_bias(meta,bias_ref,tq,npc)
    for p in range(npc):
        kv=kvs[p][...]
        kt=kv[:,:128].T
        for j in range(KVH):
            k_ref[j,p*tq:(p+1)*tq,:]=kv[:,j*HD:(j+1)*HD]
            v_ref[j,p*tq:(p+1)*tq,:]=kv[:,128+j*HD:128+(j+1)*HD]
            kT_ref[j,:,p*tq:(p+1)*tq]=kt[j*HD:(j+1)*HD,:]
    dk_ref[...]=jnp.zeros_like(dk_ref); dv_ref[...]=jnp.zeros_like(dv_ref)
    def body(i, _):
        j=i//nch; c=i%nch
        ph=lax.rem(c,3)
        cs=pl.ds(pl.multiple_of(c*CH,CH),CH)
        q=qT_ref[j,:,cs]; do=doT_ref[j,:,cs]; lse=lse_ref[j,:,cs]
        delta=jnp.sum(do.astype(F32)*oT_ref[j,:,cs],axis=0,keepdims=True)
        dq=jnp.zeros((HD,CH),F32)
        for p in range(npc):
            ks=slice(p*tq,(p+1)*tq)
            s=dot(k_ref[j,ks,:],q,NN)+bias_ref[ph,ks,:]
            pr=jnp.exp(s-lse)
            dp=dot(v_ref[j,ks,:],do,NN)
            ds=(pr*(dp-delta)).astype(BF)
            dv_ref[j,ks,:]+=dot(pr.astype(BF),do,NT)
            dk_ref[j,ks,:]+=dot(ds,q,NT)
            dq=dq+dot(kT_ref[j,:,ks],ds,NN)
        dqT_ref[j,:,cs]=dq
        return 0
    lax.fori_loop(0,KVH*nch,body,0)
    cos=cos_ref[...]; sin=sin_ref[...]; hf=HD//2
    for h in range(H):
        j,i=h//G,h%G
        a=dqT_ref[j,:hf,i*tq:(i+1)*tq]; b=dqT_ref[j,hf:,i*tq:(i+1)*tq]
        t=jnp.concatenate([a*cos+b*sin,b*cos-a*sin],axis=0)*0.125
        dq_ref[:,h*HD:(h+1)*HD]=t.T.astype(BF)
    for p in range(npc):
        ref=da_ref if p in (0,2) else db_ref
        for j in range(KVH):
            ref[p//2,:,j*HD:(j+1)*HD]=dk_ref[j,p*tq:(p+1)*tq,:].astype(BF)
            ref[p//2,:,128+j*HD:128+(j+1)*HD]=dv_ref[j,p*tq:(p+1)*tq,:].astype(BF)
def attn_bwd(meta,mid,c,dh,qT,kvs,oT,lse,wo,g2,cos,sin):
    tq=mid.shape[0]; D=mid.shape[1]; W=qT.shape[2]
    vm=pl.BlockSpec(memory_space=pltpu.VMEM)
    S=jax.ShapeDtypeStruct
    return pl.pallas_call(bwd_kernel,
        in_specs=[pl.BlockSpec(memory_space=pltpu.SMEM)]+[vm]*14, out_specs=[vm]*6,
        out_shape=[S((tq,D),F32),S((tq,D),BF),S((tq,D),BF),S((2,tq,256),BF),S((2,tq,256),BF),S((1,D),F32)],
        scratch_shapes=[pltpu.VMEM((3,4*tq,CH),F32),pltpu.VMEM((KVH,4*tq,HD),BF),pltpu.VMEM((KVH,4*tq,HD),BF),pltpu.VMEM((KVH,HD,4*tq),BF),
                        pltpu.VMEM((KVH,HD,W),BF),pltpu.VMEM((KVH,HD,W),F32),pltpu.VMEM((KVH,4*tq,HD),F32),pltpu.VMEM((KVH,4*tq,HD),F32)],
        compiler_params=pltpu.CompilerParams(vmem_limit_bytes=60<<20), name="attn_bwd")(meta,mid,c,dh,qT,*kvs,oT,lse,wo,g2,cos,sin)
def qkv_kernel(x_ref,g1_ref,w_ref,b_ref,cos_ref,sin_ref,h1_ref,qT_ref,kv_ref):
    tq=x_ref.shape[0]; hf=HD//2
    x=x_ref[...].astype(F32)
    r=lax.rsqrt(jnp.mean(x*x,axis=1,keepdims=True)+1e-6)
    h1=(x*r*g1_ref[...]).astype(BF)
    h1_ref[...]=h1
    pre=dot(h1,w_ref[...],NN)+b_ref[...]
    cos=cos_ref[...]; sin=sin_ref[...]
    kv_ref[:,128:]=pre[:,H*HD+128:].astype(BF)
    pT=pre[:,:H*HD+128].T
    def rot(h,scale):
        a=pT[h*HD:h*HD+hf,:]; b=pT[h*HD+hf:(h+1)*HD,:]
        t=jnp.concatenate([a*cos-b*sin,b*cos+a*sin],axis=0)
        return t.astype(BF)
    for h in range(H):
        j,i=h//G,h%G
        qT_ref[j,:,i*tq:(i+1)*tq]=(rot(h,1.0).astype(F32)*0.125).astype(BF)
    pad=qT_ref.shape[2]-G*tq
    if pad:
        for j in range(KVH): qT_ref[j,:,G*tq:]=jnp.zeros((HD,pad),BF)
    for j in range(KVH):
        kv_ref[:,j*HD:(j+1)*HD]=rot(H+j,1.0).T
def qkv(x,g1,w,b,cos,sin):
    tq,D=x.shape
    W=-(-G*tq//CH)*CH
    vm=pl.BlockSpec(memory_space=pltpu.VMEM); S=jax.ShapeDtypeStruct
    return pl.pallas_call(qkv_kernel,in_specs=[vm]*6,out_specs=[vm]*3,
        out_shape=[S((tq,D),BF),S((KVH,HD,W),BF),S((tq,256),BF)],
        compiler_params=pltpu.CompilerParams(vmem_limit_bytes=56<<20), name="qkv")(x,g1,w,b,cos,sin)

import math
from jax.sharding import PartitionSpec as P

THETA=1000000.0
S=jax.ShapeDtypeStruct
def ffn_kernel(mb, npc, aliased, *refs):
    hs=refs[:npc]; cs=refs[npc:2*npc]; g_ref,u_ref,d_ref=refs[2*npc:2*npc+3]
    k=2*npc+3+(5 if aliased else 0)
    hc_ref,cc_ref,hid_ref,dg_ref,du_ref,oa_ref,ob_ref,hv,cv,sem=refs[k:]
    i=pl.program_id(0)
    def cp(p):
        return (pltpu.make_async_copy(hs[p],hv.at[p],sem.at[0,p]),pltpu.make_async_copy(cs[p].at[mb],cv.at[p],sem.at[1,p]))
    @pl.when(i==0)
    def _():
        for p in range(npc):
            for c in cp(p): c.start()
    for p in range(npc):
        @pl.when(i==p)
        def _():
            for c in cp(p): c.wait()
    h=hv[i]; c=cv[i]
    hc_ref[...]=h; cc_ref[...]=c
    g=dot(h,g_ref[...],NN)
    u=dot(h,u_ref[...],NN)
    dhid=dot(c,d_ref[...],NT)
    s=jax.nn.sigmoid(g)
    a=g*s
    hid=(a*u).astype(BF)
    du=(dhid*a).astype(BF)
    dg=(dhid*u*(s*(1.0+g*(1.0-s)))).astype(BF)
    hid_ref[...]=hid; dg_ref[...]=dg; du_ref[...]=du
    o=dot(hid,d_ref[...],NN).astype(BF)
    dh=(dot(dg,g_ref[...],NT)+dot(du,u_ref[...],NT)).astype(BF)
    @pl.when(i<2)
    def _():
        oa_ref[0,0]=o; oa_ref[0,1]=dh
    @pl.when(i>=2)
    def _():
        ob_ref[0,0]=o; ob_ref[0,1]=dh
def ffn_main(mb,nmb,hs,cs,g,u,d,prev):
    npc=len(hs); tq,D=hs[0].shape; F=g.shape[1]; T=nmb*npc*tq
    anys=pl.BlockSpec(memory_space=pl.ANY)
    full=lambda a: pl.BlockSpec(a.shape, lambda i:(0,0), pipeline_mode=pl.Buffered(1))
    row=lambda w: pl.BlockSpec((tq,w), lambda i:(mb*npc+i,0))
    prev=tuple(prev) if prev is not None else ()
    al={2*npc+3+k:k for k in range(len(prev))}
    return pl.pallas_call(functools.partial(ffn_kernel,mb,npc,bool(prev)), grid=(npc,),
        in_specs=[anys]*(2*npc)+[full(g),full(u),full(d)]+[anys]*len(prev),
        out_specs=[row(D),row(D),row(F),row(F),row(F),
            pl.BlockSpec((1,2,tq,D),lambda i:(jnp.minimum(i,1),0,0,0)),
            pl.BlockSpec((1,2,tq,D),lambda i:(jnp.maximum(i-2,0),0,0,0))],
        out_shape=[S((T,D),BF),S((T,D),BF),S((T,F),BF),S((T,F),BF),S((T,F),BF),S((2,2,tq,D),BF),S((2,2,tq,D),BF)],
        scratch_shapes=[pltpu.VMEM((npc,tq,D),BF),pltpu.VMEM((npc,tq,D),BF),pltpu.SemaphoreType.DMA((2,npc))],
        input_output_aliases=al,
        compiler_params=pltpu.CompilerParams(vmem_limit_bytes=60<<20), name="ffn_main")(*hs,*cs,g,u,d,*prev)
def out_kernel(x_ref,g1_ref,w_ref,dq_ref,dkv_ref,dm_ref,cos_ref,sin_ref,dqkv_ref,ig_ref,dg1_ref,db_ref):
    hf=HD//2; qd=H*HD
    cos=cos_ref[...]; sin=sin_ref[...]
    kT=dkv_ref[:,:128].T
    rows=[]
    for j in range(KVH):
        a=kT[j*HD:j*HD+hf,:]; b=kT[j*HD+hf:(j+1)*HD,:]
        rows+=[a*cos+b*sin,b*cos-a*sin]
    dqkv_ref[:,:qd]=dq_ref[...]
    dqkv_ref[:,qd:qd+128]=jnp.concatenate(rows,axis=0).T.astype(BF)
    dqkv_ref[:,qd+128:]=dkv_ref[:,128:].astype(BF)
    dqkv=dqkv_ref[...]
    db_ref[...]=jnp.sum(dqkv.astype(F32),axis=0,keepdims=True)
    e=dot(dqkv,w_ref[...],NT)
    x=x_ref[...].astype(F32)
    r=lax.rsqrt(jnp.mean(x*x,axis=1,keepdims=True)+1e-6)
    sc=e*g1_ref[...]
    inner=jnp.mean(sc*x,axis=1,keepdims=True)
    ig_ref[...]=dm_ref[...]+r*sc-x*(r*r*r)*inner
    dg1_ref[...]=jnp.sum(e*x*r,axis=0,keepdims=True)
def out_stage(x,g1,w,dq,dkv,dm,cos,sin):
    tq,D=x.shape
    vm=pl.BlockSpec(memory_space=pltpu.VMEM)
    return pl.pallas_call(out_kernel,in_specs=[vm]*8,out_specs=[vm]*4,
        out_shape=[S((tq,w.shape[1]),BF),S((tq,D),F32),S((1,D),F32),S((1,w.shape[1]),F32)],
        compiler_params=pltpu.CompilerParams(vmem_limit_bytes=56<<20), name="out_stage")(x,g1,w,dq,dkv,dm,cos,sin)
def make(mesh):
    ND=mesh.shape["dp"]; NF=mesh.shape["fsdp"]; N=ND*NF; NX=ND//2; NZ=NF//2
    def core_swap(a): return lax.ppermute(a,"dp",[(i,i^1) for i in range(ND)])
    def x_swap(a): return lax.ppermute(a,"dp",[(i,i^2) for i in range(ND)])
    def y_swap(a): return lax.ppermute(a,"fsdp",[(i,i^1) for i in range(NF)])
    def z_perm(a,m): return lax.ppermute(a,"fsdp",[(i,i^(2*m)) for i in range(NF)])
    def pick(a,i,axis): return lax.dynamic_index_in_dim(a,i,axis,keepdims=False)
    def nat2(a,bit,axis): return jnp.where(bit==0,a,jnp.flip(a,axis))
    def addb(a,b): return (a.astype(F32)+b.astype(F32)).astype(BF)
    def per_device(layer_in,cotangent,block_doc,wq,wk,wv,wo,wg,wu,wd,bq,bk,bv,n1,n2):
        M=layer_in.shape[0]; tq=layer_in.shape[2]; D=layer_in.shape[3]; FF=wg.shape[1]
        r=wq.shape[0]; s=wd.shape[0]; kr=bk.shape[0]; QW=wq.shape[1]+wk.shape[1]+wv.shape[1]
        RB=-(-(r+1)//8)*8
        d=lax.axis_index("dp"); f=lax.axis_index("fsdp")
        X=d//2; C=d%2; Z=f//2; Y=f%2
        small=jnp.concatenate([bq,bk,bv,n1,n2])
        nsm=small.shape[0]
        smrow=jnp.pad(small,(0,QW-nsm))[None]
        A=jnp.concatenate([jnp.concatenate([wq,wk,wv],1),smrow,jnp.zeros((RB-r-1,QW),BF)],0)
        B=jnp.pad(wo,((0,RB-r),(0,0)))
        AB=jnp.concatenate([A,B],1)
        zs=jnp.stack([AB]+[z_perm(AB,m) for m in range(1,NZ)])
        A4=zs[:,:,:QW]; B4=zs[:,:,QW:]
        A8=jnp.stack([A4,x_swap(A4)]); B8=jnp.stack([B4,y_swap(B4)])
        A16=jnp.stack([A8,y_swap(A8)]); B16=jnp.stack([B8,x_swap(B8)])
        A32=jnp.stack([A16,core_swap(A16)]); B32=jnp.stack([B16,core_swap(B16)])
        b=jnp.arange(N,dtype=jnp.int32)
        bx=(b//NF)//2; bc=(b//NF)%2; bz=(b%NF)//2; by=b%2
        ia=(((bc^C)*2+(by^Y))*2+(bx^X))*NZ+(bz^Z)
        ib=(((bc^C)*2+(bx^X))*2+(by^Y))*NZ+(bz^Z)
        Wn=jnp.take(A32.reshape(N,RB,QW),ia,axis=0)
        W=Wn[:,:r].reshape(D,QW)
        sm=Wn[:,r,:nsm].astype(F32)
        WO=jnp.take(B32.reshape(N,RB,D),ib,axis=0)[:,:r].reshape(D,D)
        o=0; parts=[]
        for w_ in (r,kr,kr,r,r):
            parts.append(sm[:,o:o+w_].reshape(1,-1)); o+=w_
        bias=jnp.concatenate(parts[:3],1); g1=parts[3]; g2=parts[4]
        gu=jnp.stack([wg,wu]).reshape(2,r,NX,2,NZ,2,s).transpose(3,5,0,1,2,4,6).reshape(2,2,2,r,NX*NZ*s)
        gu=nat2(nat2(gu,C,0),Y,1)
        t=jnp.stack([gu[:,0],y_swap(gu[:,1])])
        t=jnp.stack([t[:,0],core_swap(t[:,1])])
        t=nat2(nat2(t,C,0),Y,1).transpose(2,0,1,3,4).reshape(2,4*r,NX*NZ*s)
        ixz=jnp.arange(NX*NZ,dtype=jnp.int32); ixz=((ixz//NZ)^X)*NZ+((ixz%NZ)^Z)
        def gather_xz(p):
            zz=jnp.stack([p]+[z_perm(p,m) for m in range(1,NZ)])
            return jnp.take(jnp.stack([zz,x_swap(zz)]).reshape((NX*NZ,)+p.shape),ixz,axis=0)
        def rows_nat(p): return p.reshape(NX,NZ,2,2*r,-1).transpose(0,2,1,3,4).reshape(D,-1)
        G=rows_nat(gather_xz(t[0])); U=rows_nat(gather_xz(t[1]))
        DW=gather_xz(wd).reshape(NX*NZ*s,D)
        c=cotangent[:,0]
        cy=y_swap(c)
        cs=(c,cy,core_swap(c),core_swap(cy))
        freq=jnp.exp(jnp.arange(HD//2,dtype=F32)*(-2.0*math.log(THETA)/HD))
        st=[]
        for m in range(M):
            L=jnp.sum((block_doc[m,0]==0).astype(jnp.int32))*BLK
            tok=d*tq+jnp.arange(tq,dtype=jnp.int32)
            pos=(tok-jnp.where(tok>=L,L,0)).astype(F32)
            ang=freq[:,None]*pos[None,:]
            cos=jnp.cos(ang); sin=jnp.sin(ang)
            meta=jnp.stack([d*tq,L,d*tq,(d^1)*tq,(d^2)*tq,(d^3)*tq]).astype(jnp.int32)
            x=layer_in[m,0]
            h1,qT,kv=qkv(x,g1,W,bias,cos,sin)
            kx=x_swap(kv)
            kvs=(kv,core_swap(kv),kx,core_swap(kx))
            st.append(dict(x=x,cos=cos,sin=sin,meta=meta,h1=h1,qT=qT,kvs=kvs))
        hx=[]
        for m in range(M):
            q=st[m]
            q["oT"],q["lse"],q["att"],q["mid"],h2=attn_fwd(q["meta"],q["x"],q["qT"],q["kvs"],WO,g2)
            hy=y_swap(h2)
            hx.append((h2,hy,core_swap(h2),core_swap(hy)))
        prev=None; lo=[]
        for m in range(M):
            *prev,oa,ob=ffn_main(m,M,hx[m],cs,G,U,DW,prev)
            t=addb(oa,core_swap(ob))
            fin=t[0].astype(F32)+y_swap(t[1]).astype(F32)
            lo.append((st[m]["mid"]+fin[0]).astype(BF))
            st[m]["dh"]=fin[1]
        hc,cc,hid,dg,du=prev
        def tn(a,b_): return lax.dot_general(a,b_,TN,preferred_element_type=F32)
        dD=tn(hid,cc).astype(BF).reshape(NX,NZ,s,D)
        dG=tn(hc,dg).astype(BF).reshape(NX,2,NZ,2*r,-1)
        dU=tn(hc,du).astype(BF).reshape(NX,2,NZ,2*r,-1)
        def red_xz(a,zax):
            a=addb(pick(a,X,0),x_swap(pick(a,1-X,0)))
            t=pick(a,Z,zax).astype(F32)
            for m in range(1,NZ): t=t+z_perm(pick(a,Z^m,zax),m).astype(F32)
            return t
        gD=red_xz(dD,0)
        t=jnp.stack([red_xz(dG,1),red_xz(dU,1)]).astype(BF).reshape(2,2,2,r,-1)
        t=jnp.stack([pick(t,C,1),core_swap(pick(t,1-C,1))])
        t=jnp.stack([pick(t,Y,2),y_swap(pick(t,1-Y,2))])
        t=nat2(nat2(t,Y,0),C,1).astype(F32)
        t=t.reshape(2,2,2,r,NX,NZ,s).transpose(2,3,4,1,5,0,6).reshape(2,r,FF)
        gG,gU=t[0],t[1]
        dW=None; dWO=None; ig=[]; sums=None
        for m in range(M):
            q=st[m]
            dmid,dbr,dq,da,db,dg2=attn_bwd(q["meta"],q["mid"],c[m],q["dh"],q["qT"],q["kvs"],q["oT"],q["lse"],WO,g2,q["cos"],q["sin"])
            t=addb(da,core_swap(db))
            dkv=t[0].astype(F32)+x_swap(t[1]).astype(F32)
            dqkv,igm,dg1,dbi=out_stage(q["x"],g1,W,dq,dkv,dmid,q["cos"],q["sin"])
            ig.append(igm)
            a=tn(q["h1"],dqkv); e=tn(q["att"],dbr); v=(dbi,dg1,dg2)
            dW=a if dW is None else dW+a
            dWO=e if dWO is None else dWO+e
            sums=v if sums is None else tuple(i+j for i,j in zip(sums,v))
        dbi,dg1,dg2=sums
        qd=wq.shape[1]; kd=wk.shape[1]
        sg=jnp.concatenate([dbi[0,:qd].reshape(N,r),dbi[0,qd:qd+kd].reshape(N,kr),dbi[0,qd+kd:].reshape(N,kr),dg1.reshape(N,r),dg2.reshape(N,r)],1)
        sg=jnp.pad(sg,((0,0),(0,QW-nsm)))[:,None]
        A=jnp.concatenate([dW.reshape(N,r,QW),sg,jnp.zeros((N,RB-r-1,QW),F32)],1).astype(BF).reshape(NX,2,NZ,2,RB,QW)
        B=jnp.pad(dWO.reshape(N,r,D),((0,0),(0,RB-r),(0,0))).astype(BF).reshape(NX,2,NZ,2,RB,D)
        def half(a,bit,axis,swap): return addb(pick(a,bit,axis),swap(pick(a,1-bit,axis)))
        A=half(A,C,1,core_swap); B=half(B,C,1,core_swap)
        A=half(half(A,Y,2,y_swap),X,0,x_swap); B=half(half(B,X,0,x_swap),Y,1,y_swap)
        AB=jnp.concatenate([A,B],2)
        t=pick(AB,Z,0).astype(F32)
        for m in range(1,NZ): t=t+z_perm(pick(AB,Z^m,0),m).astype(F32)
        v=t[r,:nsm]
        return (jnp.stack(lo)[:,None],jnp.stack(ig)[:,None],t[:r,:qd],t[:r,qd:qd+kd],t[:r,qd+kd:QW],t[:r,QW:],gG,gU,gD,
                v[:r],v[r:r+kr],v[r+kr:r+2*kr],v[r+2*kr:2*r+2*kr],v[2*r+2*kr:])
    return per_device
def solution(mesh):
    act=P(None,"fsdp","dp",None); row=P(("dp","fsdp"),None); vec=P(("dp","fsdp"))
    return jax.shard_map(make(mesh),mesh=mesh,
        in_specs=(act,act,P(None,"fsdp",None))+(row,)*7+(vec,)*5,
        out_specs=(act,act)+(row,)*7+(vec,)*5,check_vma=False)
```
